256 devices in a mesh: section: 8 (over y, core), chan: 32 (over z, x).
Axes of the slice: x: 4, y: 4, z: 8, core: 2. Of those that a mesh axis runs over, the one named last changes fastest.
Arguments:
- prompt: bfloat16 [192, 8192], P(None, 'chan'), may hold values from -6 to 6
- norm_gain: bfloat16 [8, 8192], P('section', 'chan'), may hold values from 0.5 to 1.5
- in_weight: bfloat16 [8, 8192, 3, 8192], P('section', None, None, 'chan'), may hold values from -0.0625 to 0.0625
- feat_taps: float32 [8, 3, 3, 8192], P('section', None, None, 'chan'), may hold values from -3 to 3
- fir_taps: float32 [8, 128, 512], P('section', None, 'chan'), may hold values from -0.5 to 0.5
- residues: float32 [8, 16, 512], P('section', None, 'chan'), may hold values from -0.2 to 0.2
- decay: float32 [8, 16, 512], P('section', None, 'chan'), may hold values from 0.002 to 0.1
Outputs:
- section_out: bfloat16 [8, 192, 8192], P('section', None, 'chan')
The draws below stay inside these ranges and needn't reach their ends.
All inputs are finite; a program needn't handle non-finite values.
Results may differ from the reference program's by a relative error of at most 0.019.
Values may be sent and summed in bfloat16 or wider, within the bound.
A program may use at most 128 MiB of HBM per device.

```python
import math
import jax
import jax.numpy as jnp
from jax import lax

D = 8192
GROUPS = 512
FIR = 128
MODES = 16
SECTIONS = 8
TOKENS = 192


def block_scale(stream_key, shape, shards, smallest, high):
    gain = 1.0
    for dim, parts in shards:
        heights = jax.random.uniform(jax.random.fold_in(jax.random.fold_in(stream_key, 6), dim), (parts,), jnp.float32, smallest / len(shards), high / len(shards))
        gain = gain * jnp.repeat(jnp.exp(heights), shape[dim] // parts).reshape((-1,) + (1,) * (len(shape) - 1 - dim))
    return gain


def scatter_about(rng, dims, deviation, limit, cuts=(), held_as=jnp.bfloat16):
    values = deviation * jax.random.normal(rng, dims, jnp.float32)
    if cuts:
        values = values * block_scale(rng, dims, cuts, -0.22, 0.18)
    return jnp.clip(values, -limit, limit).astype(held_as)


def setup_inputs(seed: int = 0) -> dict:
    keys = jax.random.split(jax.random.key(seed), 8)
    return {
        "prompt": scatter_about(keys[0], (TOKENS, D), 1.0, 6.0, ((1, 32),)),
        "norm_gain": jnp.clip(1.0 + 0.1 * jax.random.normal(keys[1], (SECTIONS, D), jnp.float32), 0.5, 1.5).astype(jnp.bfloat16),
        "in_weight": scatter_about(keys[2], (SECTIONS, D, 3, D), D ** -0.5, 0.0625, ((0, 8), (3, 32))),
        "feat_taps": scatter_about(keys[3], (SECTIONS, 3, 3, D), 0.6, 3.0, ((0, 8), (3, 32)), jnp.float32),
        "fir_taps": scatter_about(keys[4], (SECTIONS, FIR, GROUPS), 0.088, 0.5, ((0, 8), (2, 32)), jnp.float32),
        "residues": scatter_about(keys[5], (SECTIONS, MODES, GROUPS), 0.03, 0.2, ((0, 8), (2, 32)), jnp.float32),
        "decay": jnp.clip(jnp.exp(math.log(0.1) - 3.912023 * jax.random.uniform(keys[6], (SECTIONS, MODES, GROUPS), jnp.float32) ** block_scale(keys[6], (SECTIONS, MODES, GROUPS), ((0, 8), (2, 32)), -0.2, 0.2)), 0.002, 0.1),
    }


EPSILON = 1e-06

def hyena_block(inputs, gain_row, weight, tap_rows, fir_section, residue_section, decay_section, is_medium):
    length = inputs.shape[0]
    inputs_f = inputs.astype(jnp.float32)
    squares = lax.optimization_barrier(jnp.sum(inputs_f * inputs_f, axis=1, keepdims=True))
    normed = (inputs_f * lax.rsqrt(squares / D + EPSILON) * gain_row.astype(jnp.float32)).astype(jnp.bfloat16)
    projected = jnp.dot(normed, weight.reshape(D, 3 * D), preferred_element_type=jnp.float32).reshape(length, 3, D)
    padded = jnp.concatenate([jnp.zeros((2, 3, D), jnp.float32), projected], axis=0)
    features = tap_rows[0] * padded[2:] + tap_rows[1] * padded[1:-1] + tap_rows[2] * padded[:-2]
    product_kv = features[:, 1] * features[:, 2]
    if is_medium:
        filter_taps = jnp.concatenate([fir_section, jnp.zeros((length, GROUPS), jnp.float32)], axis=0)[:length]
    else:
        lag_values = jnp.arange(length).astype(jnp.float32)
        powers = jnp.exp(-decay_section[None, :, :] * lag_values[:, None, None])
        filter_taps = jnp.einsum('ng,jng->jg', residue_section, powers, precision=lax.Precision.HIGHEST)
    lag_index = jnp.arange(length)[:, None] - jnp.arange(length)[None, :]
    toeplitz = jnp.where(lag_index[None] >= 0, filter_taps.T[:, jnp.clip(lag_index, 0, length - 1)], 0.0)
    group_size = D // GROUPS
    convolved = jnp.einsum('gtp,pgk->tgk', toeplitz, product_kv.reshape(length, GROUPS, group_size), precision=lax.Precision.HIGHEST).reshape(length, D)
    return (inputs_f + features[:, 0] * convolved).astype(jnp.bfloat16)

def reference(prompt, norm_gain, in_weight, feat_taps, fir_taps, residues, decay):
    current = prompt
    outputs = []
    for section_num in range(SECTIONS):
        current = hyena_block(current, norm_gain[section_num], in_weight[section_num], feat_taps[section_num], fir_taps[section_num], residues[section_num], decay[section_num], section_num % 2 == 0)
        outputs.append(current)
    return jnp.stack(outputs)
```

```python
import functools

import jax
import jax.numpy as jnp
from jax import lax
from jax.experimental import pallas as pl
from jax.experimental.pallas import tpu as pltpu
from jax.sharding import PartitionSpec as P

MESH = pl.DeviceIdType.MESH
EPSILON = 1e-06
BLOCK = 32
XS = 4
DIRECT_FROM = 8


def ring_offsets(zs):
    offs = [0]
    for d in range(1, zs // 2 + 1):
        offs.append(d)
        if zs - d != d:
            offs.append(zs - d)
    return offs


def kernel(
    dims,
    prompt_ref, gain_ref, w_hbm, taps_ref, fir_ref, res_ref, decay_ref,
    o_ref,
    wbuf, xbuf, gbuf, gown, pbuf, fpad, gpad, tbuf, rhs,
    wsem, zsem, xsem, gsem, ssem,
):
    secs, zs, length = dims
    rows = BLOCK
    nblk = length // rows
    width = zs * XS * 256
    offs = ring_offsets(zs)
    fwd = [k for k in range(zs) if k < DIRECT_FROM]
    direct = [k for k in range(zs) if k >= DIRECT_FROM]
    sec = lax.axis_index("section")
    chan = lax.axis_index("chan")
    z = chan // XS
    x = lax.rem(chan, XS)

    def z_at(delta):
        return lax.rem(z + delta + 2 * zs, zs)

    def x_at(delta):
        return lax.rem(x + delta + 2 * XS, XS)

    def dev(s, zi, xi):
        return (s, zi * XS + xi)

    def w_copy(xr, k):
        chunk = z_at(offs[k]) * XS + x_at(xr)
        start = pl.multiple_of(chunk * 256, 256)
        return pltpu.make_async_copy(
            w_hbm.at[:, pl.ds(start, 256), :],
            wbuf.at[:, xr, pl.ds(k * 256, 256), :],
            wsem.at[xr],
        )

    for xr in range(XS):
        for k in range(zs):
            w_copy(xr, k).start()

    gown[...] = gain_ref[...].astype(jnp.float32)

    barrier = pltpu.get_barrier_semaphore()

    def hello(s, zi, xi):
        pl.semaphore_signal(barrier, inc=1, device_id=dev(s, zi, xi), device_id_type=MESH)

    for k in range(1, zs):
        hello(sec, z_at(offs[k]), x)
    for xr in range(1, XS):
        hello(sec, z, x_at(xr))

    @pl.when(sec == 0)
    def _():
        for k in direct:
            for xr in range(1, XS):
                hello(sec, z_at(offs[k]), x_at(xr))

    @pl.when(sec > 0)
    def _():
        for k in range(zs):
            hello(sec - 1, z_at(offs[k]), x)
        for k in direct:
            for xr in range(1, XS):
                hello(sec - 1, z_at(offs[k]), x_at(xr))

    greetings = zs - 1 + XS - 1
    greetings = greetings + jnp.where(sec == 0, len(direct) * (XS - 1), 0)
    greetings = greetings + jnp.where(sec < secs - 1, zs + len(direct) * (XS - 1), 0)
    pl.semaphore_wait(barrier, greetings)

    def send_block(src, target, b, own):
        for k in reversed(range(zs)):
            for xr in range(XS) if k in direct else (0,):
                sem = zsem.at[b, k] if xr == 0 else xsem.at[b, xr - 1]
                dst = xbuf.at[b, xr, k]
                if own and k == 0 and xr == 0:
                    pltpu.make_async_copy(src, dst, sem).start()
                else:
                    pltpu.make_async_remote_copy(
                        src_ref=src, dst_ref=dst,
                        send_sem=ssem.at[0 if xr == 0 else 1], recv_sem=sem,
                        device_id=dev(target, z_at(-offs[k]), x_at(-xr)), device_id_type=MESH,
                    ).start()

    @pl.when(sec == 0)
    def _():
        send_block(prompt_ref.at[pl.ds(0, rows), :], 0, 0, True)

    pltpu.make_async_copy(gown, gbuf.at[0, 0], gsem.at[0]).start()
    for k in range(1, zs):
        pltpu.make_async_remote_copy(
            src_ref=gown, dst_ref=gbuf.at[0, k], send_sem=ssem.at[3], recv_sem=gsem.at[0],
            device_id=dev(sec, z_at(-offs[k]), x), device_id_type=MESH,
        ).start()

    @pl.when(sec == 0)
    def _():
        @pl.loop(1, nblk)
        def _(b):
            start = pl.multiple_of(b * rows, rows)
            send_block(prompt_ref.at[pl.ds(start, rows), :], 0, b, True)

    pad = rows
    fpad[...] = jnp.zeros_like(fpad)
    medium = lax.rem(sec, 2) == 0

    @pl.when(medium)
    def _():
        spread = (
            lax.broadcasted_iota(jnp.int32, (16, 128), 0)
            == lax.rem(lax.broadcasted_iota(jnp.int32, (16, 128), 1), 16)
        ).astype(jnp.float32)
        taps = lax.dot_general(
            fir_ref[...], spread, (((0,), (0,)), ((), ())),
            precision=lax.Precision.HIGHEST, preferred_element_type=jnp.float32,
        )
        count = min(fir_ref.shape[1], length)
        fpad[pl.ds(pad, count), :] = taps[:count]

    @pl.when(jnp.logical_not(medium))
    def _():
        lags = lax.broadcasted_iota(jnp.int32, (length, 128), 0).astype(jnp.float32)
        res = jnp.concatenate([res_ref[...]] * 8, axis=1)
        rate = jnp.concatenate([decay_ref[...]] * 8, axis=1)
        total = jnp.zeros((length, 128), jnp.float32)
        for n in range(res.shape[0]):
            total = total + res[n : n + 1] * jnp.exp(-rate[n : n + 1] * lags)
        fpad[pl.ds(pad, length), :] = total

    span = length + rows - 8
    lane_row = lax.broadcasted_iota(jnp.int32, (1, 128), 1) // 16
    shifted = jnp.zeros((span, 128), jnp.float32)
    for i in range(8):
        shifted = jnp.where(lane_row == i, fpad[pl.ds(8 - i, span), :], shifted)
    gpad[...] = shifted
    for d in range(nblk):
        for q in range(rows // 8):
            lo = d * rows - 8 * q + rows - 8
            tbuf[d, :, pl.ds(q * 128, 128)] = gpad[pl.ds(lo, rows), :].astype(jnp.bfloat16)

    pbuf[...] = jnp.zeros_like(pbuf)

    pltpu.make_async_copy(gbuf.at[0], gbuf.at[0], gsem.at[0]).wait()
    for xr in range(1, XS):
        pltpu.make_async_remote_copy(
            src_ref=gbuf.at[0], dst_ref=gbuf.at[xr], send_sem=ssem.at[4], recv_sem=gsem.at[xr],
            device_id=dev(sec, z, x_at(-xr)), device_id_type=MESH,
        ).start()

    def forward(b):
        for k in fwd:
            pltpu.make_async_copy(xbuf.at[b, 0, k], xbuf.at[b, 0, k], zsem.at[b, k]).wait()
            for xr in (2, 1, 3):
                pltpu.make_async_remote_copy(
                    src_ref=xbuf.at[b, 0, k], dst_ref=xbuf.at[b, xr, k],
                    send_sem=ssem.at[2], recv_sem=xsem.at[b, xr - 1],
                    device_id=dev(sec, z, x_at(-xr)), device_id_type=MESH,
                ).start()

    def product(b, xr, acc, squares):
        pieces = []
        for k in range(zs):
            piece = xbuf[b, xr, k].astype(jnp.float32)
            square = piece * piece
            squares = squares + (square[:, :128] + square[:, 128:])
            pieces.append((piece * gbuf[xr, k]).astype(jnp.bfloat16))
        left = jnp.concatenate(pieces, axis=1)
        return (
            tuple(
                acc[i] + jnp.dot(left, wbuf[i, xr], preferred_element_type=jnp.float32)
                for i in range(3)
            ),
            squares,
        )

    lane_group = lax.broadcasted_iota(jnp.int32, (16, 256), 1) // 16
    own_group = lane_group == lax.broadcasted_iota(jnp.int32, (16, 256), 0)

    forward(0)
    for xr in range(XS):
        pltpu.make_async_copy(wbuf.at[:, xr], wbuf.at[:, xr], wsem.at[xr]).wait()
    for xr in range(1, XS):
        pltpu.make_async_copy(gbuf.at[xr], gbuf.at[xr], gsem.at[xr]).wait()

    def block(b, carry):
        def earlier(d, total):
            return total + jnp.dot(tbuf[d], rhs[b - d], preferred_element_type=jnp.float32)

        conv = lax.fori_loop(1, b + 1, earlier, jnp.zeros((rows, 256), jnp.float32))
        for k in direct:
            pltpu.make_async_copy(xbuf.at[b, 0, k], xbuf.at[b, 0, k], zsem.at[b, k]).wait()
        acc = tuple(jnp.zeros((rows, 256), jnp.float32) for i in range(3))
        acc, squares = product(b, 0, acc, jnp.zeros((rows, 128), jnp.float32))

        def side(xr, state):
            pltpu.make_async_copy(xbuf.at[b, xr], xbuf.at[b, xr], xsem.at[b, xr - 1]).wait()
            return product(b, xr, *state)

        acc, squares = lax.fori_loop(1, XS, side, (acc, squares))
        scale = lax.rsqrt(jnp.sum(squares, axis=1, keepdims=True) / width + EPSILON)
        feats = []
        for i in range(3):
            pbuf[i, pl.ds(8, rows), :] = acc[i] * scale
            feats.append(
                taps_ref[i] * pbuf[i, pl.ds(8, rows), :]
                + taps_ref[3 + i] * pbuf[i, pl.ds(7, rows), :]
                + taps_ref[6 + i] * pbuf[i, pl.ds(6, rows), :]
            )
        kv = feats[1] * feats[2]
        for p in range(rows):
            rhs[b, pl.ds(p * 16, 16), :] = jnp.where(
                own_group, jnp.broadcast_to(kv[p : p + 1], (16, 256)), 0.0
            ).astype(jnp.bfloat16)
        conv = conv + jnp.dot(tbuf[0], rhs[b], preferred_element_type=jnp.float32)
        start = pl.multiple_of(b * rows, rows)
        result = xbuf[b, 0, 0].astype(jnp.float32) + feats[0] * conv
        o_ref[pl.ds(start, rows), :] = result.astype(jnp.bfloat16)

        @pl.when(sec < secs - 1)
        def _():
            send_block(o_ref.at[pl.ds(start, rows), :], sec + 1, b, False)

        for i in range(3):
            pbuf[i, pl.ds(0, 8), :] = pbuf[i, pl.ds(rows, 8), :]

        @pl.when(b < nblk - 1)
        def _():
            forward(b + 1)

        return carry

    lax.fori_loop(0, nblk, block, 0)

    def sent(view, which):
        pltpu.make_async_copy(view, view, ssem.at[which]).wait()

    @pl.when(sec == 0)
    def _():
        sent(xbuf.at[:, 0, pl.ds(1, zs - 1)], 0)
        if direct:
            sent(xbuf.at[:, pl.ds(1, XS - 1), pl.ds(0, len(direct))], 1)

    @pl.when(sec < secs - 1)
    def _():
        sent(xbuf.at[:, 0], 0)
        if direct:
            sent(xbuf.at[:, pl.ds(1, XS - 1), pl.ds(0, len(direct))], 1)

    if fwd:
        sent(xbuf.at[:, pl.ds(1, XS - 1), pl.ds(0, len(fwd))], 2)
    sent(gbuf.at[0, pl.ds(1, zs - 1)], 3)
    sent(gbuf.at[pl.ds(1, XS - 1)], 4)


def solution(mesh):
    secs = mesh.shape["section"]
    zs = mesh.shape["chan"] // XS

    def body(prompt, norm_gain, in_weight, feat_taps, fir_taps, residues, decay):
        length, local = prompt.shape
        rows = BLOCK
        nblk = length // rows
        vmem = pl.BlockSpec(memory_space=pltpu.VMEM)
        out = pl.pallas_call(
            functools.partial(kernel, (secs, zs, length)),
            name="relay",
            out_shape=jax.ShapeDtypeStruct((length, local), jnp.bfloat16),
            in_specs=[vmem, vmem, pl.BlockSpec(memory_space=pl.ANY), vmem, vmem, vmem, vmem],
            out_specs=vmem,
            scratch_shapes=[
                pltpu.VMEM((3, XS, zs * 256, 256), jnp.bfloat16),
                pltpu.VMEM((nblk, XS, zs, rows, 256), jnp.bfloat16),
                pltpu.VMEM((XS, zs, 1, 256), jnp.float32),
                pltpu.VMEM((1, 256), jnp.float32),
                pltpu.VMEM((3, 8 + rows, 256), jnp.float32),
                pltpu.VMEM((rows + length, 128), jnp.float32),
                pltpu.VMEM((rows + length - 8, 128), jnp.float32),
                pltpu.VMEM((nblk, rows, rows * 16), jnp.bfloat16),
                pltpu.VMEM((nblk, rows * 16, 256), jnp.bfloat16),
                pltpu.SemaphoreType.DMA((XS,)),
                pltpu.SemaphoreType.DMA((nblk, zs)),
                pltpu.SemaphoreType.DMA((nblk, XS - 1)),
                pltpu.SemaphoreType.DMA((XS,)),
                pltpu.SemaphoreType.DMA((5,)),
            ],
            compiler_params=pltpu.CompilerParams(
                collective_id=0, has_side_effects=True, vmem_limit_bytes=56 << 20
            ),
        )(
            prompt,
            norm_gain,
            in_weight[0].transpose(1, 0, 2),
            feat_taps[0].reshape(9, 1, local),
            fir_taps[0].T,
            residues[0],
            decay[0],
        )
        return out[None]

    return jax.shard_map(
        body,
        mesh=mesh,
        in_specs=(
            P(None, "chan"),
            P("section", "chan"),
            P("section", None, None, "chan"),
            P("section", None, None, "chan"),
            P("section", None, "chan"),
            P("section", None, "chan"),
            P("section", None, "chan"),
        ),
        out_specs=P("section", None, "chan"),
        check_vma=False,
    )
```

```python
import functools

import jax
import jax.numpy as jnp
from jax import lax
from jax.experimental import pallas as pl
from jax.experimental.pallas import tpu as pltpu
from jax.sharding import PartitionSpec as P

MESH = pl.DeviceIdType.MESH
EPSILON = 1e-06
BLOCK = 16
XS = 4
DIRECT_FROM = 8
LOOK = 0
DEPTH = 2
ORDER = (7, 6, 5, 4, 3, 2, 1, 0)
UNROLL = 4
MERGE = ((0,), (1, 2), (3, 4), (5, 6), (7,))


def ring_offsets(zs):
    offs = [0]
    for d in range(1, zs // 2 + 1):
        offs.append(d)
        if zs - d != d:
            offs.append(zs - d)
    return offs


def kernel(
    dims,
    prompt_ref, gain_ref, w_hbm, taps_ref, fir_ref, res_ref, decay_ref,
    o_ref,
    wbuf, xbuf, gbuf, gown, pbuf, fpad, gpad, tbuf, rhs,
    wsem, zsem, xsem, gsem, ssem,
):
    secs, zs, length = dims
    rows = BLOCK
    nblk = length // rows
    width = zs * XS * 256
    offs = ring_offsets(zs)
    fwd = [k for k in range(zs) if k < DIRECT_FROM]
    direct = [k for k in range(zs) if k >= DIRECT_FROM]
    sec = lax.axis_index("section")
    chan = lax.axis_index("chan")
    z = chan // XS
    x = lax.rem(chan, XS)

    def z_at(delta):
        return lax.rem(z + delta + 2 * zs, zs)

    def x_at(delta):
        return lax.rem(x + delta + 2 * XS, XS)

    def dev(s, zi, xi):
        return (s, zi * XS + xi)

    def w_copy(xr, k):
        chunk = z_at(offs[k]) * XS + x_at(xr)
        start = pl.multiple_of(chunk * 256, 256)
        return pltpu.make_async_copy(
            w_hbm.at[:, pl.ds(start, 256), :],
            wbuf.at[:, xr, pl.ds(k * 256, 256), :],
            wsem.at[xr],
        )

    gown[...] = gain_ref[...].astype(jnp.float32)

    barrier = pltpu.get_barrier_semaphore()

    def hello(s, zi, xi):
        pl.semaphore_signal(barrier, inc=1, device_id=dev(s, zi, xi), device_id_type=MESH)

    for k in range(1, zs):
        hello(sec, z_at(offs[k]), x)
    for xr in range(1, XS):
        hello(sec, z, x_at(xr))

    @pl.when(sec == 0)
    def _():
        for k in direct:
            for xr in range(1, XS):
                hello(sec, z_at(offs[k]), x_at(xr))

    @pl.when(sec > 0)
    def _():
        for k in range(zs):
            hello(sec - 1, z_at(offs[k]), x)
        for k in direct:
            for xr in range(1, XS):
                hello(sec - 1, z_at(offs[k]), x_at(xr))

    for xr in range(XS):
        for k in range(zs):
            w_copy(xr, k).start()

    greetings = zs - 1 + XS - 1
    greetings = greetings + jnp.where(sec == 0, len(direct) * (XS - 1), 0)
    greetings = greetings + jnp.where(sec < secs - 1, zs + len(direct) * (XS - 1), 0)
    pl.semaphore_wait(barrier, greetings)

    def send_block(src, target, b, own):
        for k in ORDER or range(zs):
            for xr in (2, 1, 3, 0) if k in direct else (0,):
                sem = zsem.at[b, k] if xr == 0 else xsem.at[b, xr - 1]
                dst = xbuf.at[b, xr, k]
                if own and k == 0 and xr == 0:
                    pltpu.make_async_copy(src, dst, sem).start()
                else:
                    pltpu.make_async_remote_copy(
                        src_ref=src, dst_ref=dst,
                        send_sem=ssem.at[0 if xr == 0 else 1], recv_sem=sem,
                        device_id=dev(target, z_at(-offs[k]), x_at(-xr)), device_id_type=MESH,
                    ).start()

    ahead = min(DEPTH + 1, nblk)

    @pl.when(sec == 0)
    def _():
        for b in range(ahead):
            send_block(prompt_ref.at[pl.ds(b * rows, rows), :], 0, b, True)

    pltpu.make_async_copy(gown, gbuf.at[0, 0], gsem.at[0]).start()
    for k in range(1, zs):
        pltpu.make_async_remote_copy(
            src_ref=gown, dst_ref=gbuf.at[0, k], send_sem=ssem.at[3], recv_sem=gsem.at[0],
            device_id=dev(sec, z_at(-offs[k]), x), device_id_type=MESH,
        ).start()

    pad = rows
    fpad[...] = jnp.zeros_like(fpad)
    medium = lax.rem(sec, 2) == 0

    @pl.when(medium)
    def _():
        spread = (
            lax.broadcasted_iota(jnp.int32, (16, 128), 0)
            == lax.rem(lax.broadcasted_iota(jnp.int32, (16, 128), 1), 16)
        ).astype(jnp.float32)
        taps = lax.dot_general(
            fir_ref[...], spread, (((0,), (0,)), ((), ())),
            precision=lax.Precision.HIGHEST, preferred_element_type=jnp.float32,
        )
        count = min(fir_ref.shape[1], length)
        fpad[pl.ds(pad, count), :] = taps[:count]

    @pl.when(jnp.logical_not(medium))
    def _():
        lags = lax.broadcasted_iota(jnp.int32, (length, 128), 0).astype(jnp.float32)
        res = jnp.concatenate([res_ref[...]] * 8, axis=1)
        rate = jnp.concatenate([decay_ref[...]] * 8, axis=1)
        total = jnp.zeros((length, 128), jnp.float32)
        for n in range(res.shape[0]):
            total = total + res[n : n + 1] * jnp.exp(-rate[n : n + 1] * lags)
        fpad[pl.ds(pad, length), :] = total

    span = length + rows - 8
    lane_row = lax.broadcasted_iota(jnp.int32, (1, 128), 1) // 16
    shifted = jnp.zeros((span, 128), jnp.float32)
    for i in range(8):
        shifted = jnp.where(lane_row == i, fpad[pl.ds(8 - i, span), :], shifted)
    gpad[...] = shifted
    for d in range(nblk):
        for q in range(rows // 8):
            lo = d * rows - 8 * q + rows - 8
            tbuf[d, :, pl.ds(q * 128, 128)] = gpad[pl.ds(lo, rows), :].astype(jnp.bfloat16)

    for d in range(UNROLL - 1):
        tbuf[nblk + d] = jnp.zeros(tbuf.shape[1:], jnp.bfloat16)
        rhs[d] = jnp.zeros(rhs.shape[1:], jnp.bfloat16)
    pbuf[...] = jnp.zeros_like(pbuf)

    def forward(b):
        for group in MERGE:
            group = [k for k in group if k in fwd]
            if not group:
                continue
            for k in group:
                pltpu.make_async_copy(xbuf.at[b, 0, k], xbuf.at[b, 0, k], zsem.at[b, k]).wait()
            part = pl.ds(group[0], len(group))
            for xr in (2, 1, 3):
                pltpu.make_async_remote_copy(
                    src_ref=xbuf.at[b, 0, part], dst_ref=xbuf.at[b, xr, part],
                    send_sem=ssem.at[2], recv_sem=xsem.at[b, xr - 1],
                    device_id=dev(sec, z, x_at(-xr)), device_id_type=MESH,
                ).start()

    def forward_next(b, place):
        if place == LOOK:
            then = b + jnp.where(sec == 0, DEPTH, 1)

            @pl.when(then < nblk)
            def _():
                forward(then)

    def product(b, xr, acc, squares):
        pieces = []
        for k in range(zs):
            piece = xbuf[b, xr, k].astype(jnp.float32)
            square = piece * piece
            squares = squares + (square[:, :128] + square[:, 128:])
            pieces.append((piece * gbuf[xr, k]).astype(jnp.bfloat16))
        left = jnp.concatenate(pieces, axis=1)
        return (
            tuple(
                acc[i] + jnp.dot(left, wbuf[i, xr], preferred_element_type=jnp.float32)
                for i in range(3)
            ),
            squares,
        )

    lane_group = lax.broadcasted_iota(jnp.int32, (16, 256), 1) // 16
    own_group = lane_group == lax.broadcasted_iota(jnp.int32, (16, 256), 0)

    def spread_gains():
        pltpu.make_async_copy(gbuf.at[0], gbuf.at[0], gsem.at[0]).wait()
        for xr in range(1, XS):
            pltpu.make_async_remote_copy(
                src_ref=gbuf.at[0], dst_ref=gbuf.at[xr], send_sem=ssem.at[4], recv_sem=gsem.at[xr],
                device_id=dev(sec, z, x_at(-xr)), device_id_type=MESH,
            ).start()

    @pl.when(sec > 0)
    def _():
        spread_gains()

    forward(0)

    @pl.when(sec == 0)
    def _():
        spread_gains()
        for b in range(1, min(DEPTH, nblk)):
            forward(b)

    @pl.when(sec == 0)
    def _():
        @pl.loop(ahead, nblk)
        def _(b):
            start = pl.multiple_of(b * rows, rows)
            send_block(prompt_ref.at[pl.ds(start, rows), :], 0, b, True)

    for xr in range(XS):
        pltpu.make_async_copy(wbuf.at[:, xr], wbuf.at[:, xr], wsem.at[xr]).wait()
    for xr in range(1, XS):
        pltpu.make_async_copy(gbuf.at[xr], gbuf.at[xr], gsem.at[xr]).wait()

    def block(b, carry):
        def earlier(step, total):
            for i in range(UNROLL):
                d = 1 + step * UNROLL + i
                total = total + jnp.dot(
                    tbuf[d], rhs[b - d + UNROLL - 1], preferred_element_type=jnp.float32
                )
            return total

        conv = lax.fori_loop(
            0, (b + UNROLL - 1) // UNROLL, earlier, jnp.zeros((rows, 256), jnp.float32)
        )
        for k in direct:
            pltpu.make_async_copy(xbuf.at[b, 0, k], xbuf.at[b, 0, k], zsem.at[b, k]).wait()
        acc = tuple(jnp.zeros((rows, 256), jnp.float32) for i in range(3))
        state = product(b, 0, acc, jnp.zeros((rows, 128), jnp.float32))
        forward_next(b, 0)
        for place, xr in enumerate((1, 3, 2)):
            pltpu.make_async_copy(xbuf.at[b, xr], xbuf.at[b, xr], xsem.at[b, xr - 1]).wait()
            state = product(b, xr, *state)
            forward_next(b, place + 1)
        acc, squares = state
        scale = lax.rsqrt(jnp.sum(squares, axis=1, keepdims=True) / width + EPSILON)
        feats = []
        for i in range(3):
            pbuf[i, pl.ds(8, rows), :] = acc[i] * scale
            feats.append(
                taps_ref[i] * pbuf[i, pl.ds(8, rows), :]
                + taps_ref[3 + i] * pbuf[i, pl.ds(7, rows), :]
                + taps_ref[6 + i] * pbuf[i, pl.ds(6, rows), :]
            )
        kv = feats[1] * feats[2]
        for p in range(rows):
            rhs[b + UNROLL - 1, pl.ds(p * 16, 16), :] = jnp.where(
                own_group, jnp.broadcast_to(kv[p : p + 1], (16, 256)), 0.0
            ).astype(jnp.bfloat16)
        conv = conv + jnp.dot(tbuf[0], rhs[b + UNROLL - 1], preferred_element_type=jnp.float32)
        start = pl.multiple_of(b * rows, rows)
        result = xbuf[b, 0, 0].astype(jnp.float32) + feats[0] * conv
        o_ref[pl.ds(start, rows), :] = result.astype(jnp.bfloat16)

        @pl.when(sec < secs - 1)
        def _():
            send_block(o_ref.at[pl.ds(start, rows), :], sec + 1, b, False)

        for i in range(3):
            pbuf[i, pl.ds(0, 8), :] = pbuf[i, pl.ds(rows, 8), :]

        forward_next(b, 4)
        return carry

    lax.fori_loop(0, nblk, block, 0)

    def sent(view, which):
        pltpu.make_async_copy(view, view, ssem.at[which]).wait()

    @pl.when(sec == 0)
    def _():
        sent(xbuf.at[:, 0, pl.ds(1, zs - 1)], 0)
        if direct:
            sent(xbuf.at[:, pl.ds(1, XS - 1), pl.ds(0, len(direct))], 1)

    @pl.when(sec < secs - 1)
    def _():
        sent(xbuf.at[:, 0], 0)
        if direct:
            sent(xbuf.at[:, pl.ds(1, XS - 1), pl.ds(0, len(direct))], 1)

    if fwd:
        sent(xbuf.at[:, pl.ds(1, XS - 1), pl.ds(0, len(fwd))], 2)
    sent(gbuf.at[0, pl.ds(1, zs - 1)], 3)
    sent(gbuf.at[pl.ds(1, XS - 1)], 4)


def solution(mesh):
    secs = mesh.shape["section"]
    zs = mesh.shape["chan"] // XS

    def body(prompt, norm_gain, in_weight, feat_taps, fir_taps, residues, decay):
        length, local = prompt.shape
        rows = BLOCK
        nblk = length // rows
        vmem = pl.BlockSpec(memory_space=pltpu.VMEM)
        out = pl.pallas_call(
            functools.partial(kernel, (secs, zs, length)),
            name="relay",
            out_shape=jax.ShapeDtypeStruct((length, local), jnp.bfloat16),
            in_specs=[vmem, vmem, pl.BlockSpec(memory_space=pl.ANY), vmem, vmem, vmem, vmem],
            out_specs=vmem,
            scratch_shapes=[
                pltpu.VMEM((3, XS, zs * 256, 256), jnp.bfloat16),
                pltpu.VMEM((nblk, XS, zs, rows, 256), jnp.bfloat16),
                pltpu.VMEM((XS, zs, 1, 256), jnp.float32),
                pltpu.VMEM((1, 256), jnp.float32),
                pltpu.VMEM((3, 8 + rows, 256), jnp.float32),
                pltpu.VMEM((rows + length, 128), jnp.float32),
                pltpu.VMEM((rows + length - 8, 128), jnp.float32),
                pltpu.VMEM((nblk + UNROLL - 1, rows, rows * 16), jnp.bfloat16),
                pltpu.VMEM((nblk + UNROLL - 1, rows * 16, 256), jnp.bfloat16),
                pltpu.SemaphoreType.DMA((XS,)),
                pltpu.SemaphoreType.DMA((nblk, zs)),
                pltpu.SemaphoreType.DMA((nblk, XS - 1)),
                pltpu.SemaphoreType.DMA((XS,)),
                pltpu.SemaphoreType.DMA((5,)),
            ],
            compiler_params=pltpu.CompilerParams(
                collective_id=0, has_side_effects=True, vmem_limit_bytes=56 << 20
            ),
        )(
            prompt,
            norm_gain,
            in_weight[0].transpose(1, 0, 2),
            feat_taps[0].reshape(9, 1, local),
            fir_taps[0].T,
            residues[0],
            decay[0],
        )
        return out[None]

    return jax.shard_map(
        body,
        mesh=mesh,
        in_specs=(
            P(None, "chan"),
            P("section", "chan"),
            P("section", None, None, "chan"),
            P("section", None, None, "chan"),
            P("section", None, "chan"),
            P("section", None, "chan"),
            P("section", None, "chan"),
        ),
        out_specs=P("section", None, "chan"),
        check_vma=False,
    )
```

```python
import functools

import jax
import jax.numpy as jnp
from jax import lax
from jax.experimental import pallas as pl
from jax.experimental.pallas import tpu as pltpu
from jax.sharding import PartitionSpec as P

MESH = pl.DeviceIdType.MESH
EPSILON = 1e-06
BLOCK = 16
XS = 4
LOOK = 0
DEPTH = 2
ORDER = (0, 7, 6, 5, 4, 3, 2, 1)
UNROLL = 4
MERGE = ((0,), (1, 2), (3, 4), (5, 6), (7,))


def ring_offsets(zs):
    offs = [0]
    for d in range(1, zs // 2 + 1):
        offs.append(d)
        if zs - d != d:
            offs.append(zs - d)
    return offs


def kernel(
    dims,
    prompt_ref, gain_ref, w_hbm, taps_ref, fir_ref, res_ref, decay_ref,
    o_ref,
    wbuf, xbuf, gbuf, gown, pbuf, fpad, gpad, tbuf, rhs,
    wsem, zsem, xsem, gsem, ssem,
):
    secs, zs, length = dims
    rows = BLOCK
    nblk = length // rows
    width = zs * XS * 256
    offs = ring_offsets(zs)
    sec = lax.axis_index("section")
    chan = lax.axis_index("chan")
    z = chan // XS
    x = lax.rem(chan, XS)

    def z_at(delta):
        return lax.rem(z + delta + 2 * zs, zs)

    def x_at(delta):
        return lax.rem(x + delta + 2 * XS, XS)

    def dev(s, zi, xi):
        return (s, zi * XS + xi)

    def w_copy(xr, k):
        chunk = z_at(offs[k]) * XS + x_at(xr)
        start = pl.multiple_of(chunk * 256, 256)
        return pltpu.make_async_copy(
            w_hbm.at[:, pl.ds(start, 256), :],
            wbuf.at[:, xr, pl.ds(k * 256, 256), :],
            wsem.at[xr],
        )

    gown[...] = gain_ref[...].astype(jnp.float32)

    barrier = pltpu.get_barrier_semaphore()

    def hello(s, zi, xi):
        pl.semaphore_signal(barrier, inc=1, device_id=dev(s, zi, xi), device_id_type=MESH)

    for k in range(1, zs):
        hello(sec, z_at(offs[k]), x)
    for xr in range(1, XS):
        hello(sec, z, x_at(xr))

    @pl.when(sec == 0)
    def _():
        for k in range(zs):
            hello(1, z_at(offs[k]), x)

    @pl.when(sec > 0)
    def _():
        for k in range(zs):
            hello(sec - 1, z_at(offs[k]), x)

    for xr in range(XS):
        for k in range(zs):
            w_copy(xr, k).start()

    greetings = zs - 1 + XS - 1
    greetings = greetings + jnp.where(sec < secs - 1, zs, 0)
    greetings = greetings + jnp.where(sec == 1, zs, 0)
    pl.semaphore_wait(barrier, greetings)

    column = [z_at(-offs[k]) * XS + x for k in range(zs)]
    across = [z * XS + x_at(-xr) for xr in range(XS)]

    def send_block(src, target, b, own):
        for k in ORDER:
            dst, sem = xbuf.at[b, 0, k], zsem.at[b, k]
            if own and k == 0:
                pltpu.make_async_copy(src, dst, sem).start()
            else:
                pltpu.make_async_remote_copy(
                    src_ref=src, dst_ref=dst, send_sem=ssem.at[0], recv_sem=sem,
                    device_id=(target, column[k]), device_id_type=MESH,
                ).start()

    pltpu.make_async_copy(gown, gbuf.at[0, 0], gsem.at[0]).start()
    for k in range(1, zs):
        pltpu.make_async_remote_copy(
            src_ref=gown, dst_ref=gbuf.at[0, k], send_sem=ssem.at[2], recv_sem=gsem.at[0],
            device_id=dev(sec, z_at(-offs[k]), x), device_id_type=MESH,
        ).start()

    @pl.when(sec == 0)
    def _():
        send_block(prompt_ref.at[pl.ds(0, rows), :], 0, 0, True)

    @pl.when(sec == 1)
    def _():
        @pl.loop(1, nblk)
        def _(b):
            start = pl.multiple_of(b * rows, rows)
            send_block(prompt_ref.at[pl.ds(start, rows), :], 0, b, False)

    pad = rows
    fpad[...] = jnp.zeros_like(fpad)
    medium = lax.rem(sec, 2) == 0

    @pl.when(medium)
    def _():
        spread = (
            lax.broadcasted_iota(jnp.int32, (16, 128), 0)
            == lax.rem(lax.broadcasted_iota(jnp.int32, (16, 128), 1), 16)
        ).astype(jnp.float32)
        taps = lax.dot_general(
            fir_ref[...], spread, (((0,), (0,)), ((), ())),
            precision=lax.Precision.HIGHEST, preferred_element_type=jnp.float32,
        )
        count = min(fir_ref.shape[1], length)
        fpad[pl.ds(pad, count), :] = taps[:count]

    @pl.when(jnp.logical_not(medium))
    def _():
        lags = lax.broadcasted_iota(jnp.int32, (length, 128), 0).astype(jnp.float32)
        res = jnp.concatenate([res_ref[...]] * 8, axis=1)
        rate = jnp.concatenate([decay_ref[...]] * 8, axis=1)
        total = jnp.zeros((length, 128), jnp.float32)
        for n in range(res.shape[0]):
            total = total + res[n : n + 1] * jnp.exp(-rate[n : n + 1] * lags)
        fpad[pl.ds(pad, length), :] = total

    span = length + rows - 8
    lane_row = lax.broadcasted_iota(jnp.int32, (1, 128), 1) // 16
    shifted = jnp.zeros((span, 128), jnp.float32)
    for i in range(8):
        shifted = jnp.where(lane_row == i, fpad[pl.ds(8 - i, span), :], shifted)
    gpad[...] = shifted
    for d in range(nblk):
        for q in range(rows // 8):
            lo = d * rows - 8 * q + rows - 8
            tbuf[d, :, pl.ds(q * 128, 128)] = gpad[pl.ds(lo, rows), :].astype(jnp.bfloat16)

    for d in range(UNROLL - 1):
        tbuf[nblk + d] = jnp.zeros(tbuf.shape[1:], jnp.bfloat16)
        rhs[d] = jnp.zeros(rhs.shape[1:], jnp.bfloat16)
    pbuf[...] = jnp.zeros_like(pbuf)

    def forward(b):
        for group in MERGE:
            for k in group:
                pltpu.make_async_copy(xbuf.at[b, 0, k], xbuf.at[b, 0, k], zsem.at[b, k]).wait()
            part = pl.ds(group[0], len(group))
            for xr in (2, 1, 3):
                pltpu.make_async_remote_copy(
                    src_ref=xbuf.at[b, 0, part], dst_ref=xbuf.at[b, xr, part],
                    send_sem=ssem.at[1], recv_sem=xsem.at[b, xr - 1],
                    device_id=(sec, across[xr]), device_id_type=MESH,
                ).start()

    def forward_next(b, place):
        if place == LOOK:
            then = b + jnp.where(sec == 0, DEPTH, 1)

            @pl.when(then < nblk)
            def _():
                forward(then)

    def product(b, xr, acc, squares):
        pieces = []
        for k in range(zs):
            piece = xbuf[b, xr, k].astype(jnp.float32)
            square = piece * piece
            squares = squares + (square[:, :128] + square[:, 128:])
            pieces.append((piece * gbuf[xr, k]).astype(jnp.bfloat16))
        left = jnp.concatenate(pieces, axis=1)
        return (
            tuple(
                acc[i] + jnp.dot(left, wbuf[i, xr], preferred_element_type=jnp.float32)
                for i in range(3)
            ),
            squares,
        )

    lane_group = lax.broadcasted_iota(jnp.int32, (16, 256), 1) // 16
    own_group = lane_group == lax.broadcasted_iota(jnp.int32, (16, 256), 0)

    pltpu.make_async_copy(gbuf.at[0], gbuf.at[0], gsem.at[0]).wait()
    for xr in range(1, XS):
        pltpu.make_async_remote_copy(
            src_ref=gbuf.at[0], dst_ref=gbuf.at[xr], send_sem=ssem.at[3], recv_sem=gsem.at[xr],
            device_id=dev(sec, z, x_at(-xr)), device_id_type=MESH,
        ).start()

    forward(0)

    @pl.when(sec == 0)
    def _():
        for b in range(1, min(DEPTH, nblk)):
            forward(b)

    for xr in range(XS):
        pltpu.make_async_copy(wbuf.at[:, xr], wbuf.at[:, xr], wsem.at[xr]).wait()
    for xr in range(1, XS):
        pltpu.make_async_copy(gbuf.at[xr], gbuf.at[xr], gsem.at[xr]).wait()

    def block(b, carry):
        def earlier(step, total):
            for i in range(UNROLL):
                d = 1 + step * UNROLL + i
                total = total + jnp.dot(
                    tbuf[d], rhs[b - d + UNROLL - 1], preferred_element_type=jnp.float32
                )
            return total

        conv = lax.fori_loop(
            0, (b + UNROLL - 1) // UNROLL, earlier, jnp.zeros((rows, 256), jnp.float32)
        )
        acc = tuple(jnp.zeros((rows, 256), jnp.float32) for i in range(3))
        state = product(b, 0, acc, jnp.zeros((rows, 128), jnp.float32))
        forward_next(b, 0)
        for place, xr in enumerate((1, 3, 2)):
            pltpu.make_async_copy(xbuf.at[b, xr], xbuf.at[b, xr], xsem.at[b, xr - 1]).wait()
            state = product(b, xr, *state)
            forward_next(b, place + 1)
        acc, squares = state
        scale = lax.rsqrt(jnp.sum(squares, axis=1, keepdims=True) / width + EPSILON)
        feats = []
        for i in range(3):
            pbuf[i, pl.ds(8, rows), :] = acc[i] * scale
            feats.append(
                taps_ref[i] * pbuf[i, pl.ds(8, rows), :]
                + taps_ref[3 + i] * pbuf[i, pl.ds(7, rows), :]
                + taps_ref[6 + i] * pbuf[i, pl.ds(6, rows), :]
            )
        kv = feats[1] * feats[2]
        for p in range(rows):
            rhs[b + UNROLL - 1, pl.ds(p * 16, 16), :] = jnp.where(
                own_group, jnp.broadcast_to(kv[p : p + 1], (16, 256)), 0.0
            ).astype(jnp.bfloat16)
        conv = conv + jnp.dot(tbuf[0], rhs[b + UNROLL - 1], preferred_element_type=jnp.float32)
        start = pl.multiple_of(b * rows, rows)
        result = xbuf[b, 0, 0].astype(jnp.float32) + feats[0] * conv
        o_ref[pl.ds(start, rows), :] = result.astype(jnp.bfloat16)

        @pl.when(sec < secs - 1)
        def _():
            send_block(o_ref.at[pl.ds(start, rows), :], sec + 1, b, False)

        for i in range(3):
            pbuf[i, pl.ds(0, 8), :] = pbuf[i, pl.ds(rows, 8), :]

        forward_next(b, 4)
        return carry

    lax.fori_loop(0, nblk, block, 0)

    def sent(view, which):
        pltpu.make_async_copy(view, view, ssem.at[which]).wait()

    @pl.when(sec == 0)
    def _():
        sent(xbuf.at[0, 0, pl.ds(1, zs - 1)], 0)

    @pl.when(sec == 1)
    def _():
        sent(xbuf.at[pl.ds(1, nblk - 1), 0], 0)

    @pl.when(sec < secs - 1)
    def _():
        sent(xbuf.at[:, 0], 0)

    sent(xbuf.at[:, pl.ds(1, XS - 1)], 1)
    sent(gbuf.at[0, pl.ds(1, zs - 1)], 2)
    sent(gbuf.at[pl.ds(1, XS - 1)], 3)


def solution(mesh):
    secs = mesh.shape["section"]
    zs = mesh.shape["chan"] // XS

    def body(prompt, norm_gain, in_weight, feat_taps, fir_taps, residues, decay):
        length, local = prompt.shape
        rows = BLOCK
        nblk = length // rows
        vmem = pl.BlockSpec(memory_space=pltpu.VMEM)
        out = pl.pallas_call(
            functools.partial(kernel, (secs, zs, length)),
            name="relay",
            out_shape=jax.ShapeDtypeStruct((length, local), jnp.bfloat16),
            in_specs=[vmem, vmem, pl.BlockSpec(memory_space=pl.ANY), vmem, vmem, vmem, vmem],
            out_specs=vmem,
            scratch_shapes=[
                pltpu.VMEM((3, XS, zs * 256, 256), jnp.bfloat16),
                pltpu.VMEM((nblk, XS, zs, rows, 256), jnp.bfloat16),
                pltpu.VMEM((XS, zs, 1, 256), jnp.float32),
                pltpu.VMEM((1, 256), jnp.float32),
                pltpu.VMEM((3, 8 + rows, 256), jnp.float32),
                pltpu.VMEM((rows + length, 128), jnp.float32),
                pltpu.VMEM((rows + length - 8, 128), jnp.float32),
                pltpu.VMEM((nblk + UNROLL - 1, rows, rows * 16), jnp.bfloat16),
                pltpu.VMEM((nblk + UNROLL - 1, rows * 16, 256), jnp.bfloat16),
                pltpu.SemaphoreType.DMA((XS,)),
                pltpu.SemaphoreType.DMA((nblk, zs)),
                pltpu.SemaphoreType.DMA((nblk, XS - 1)),
                pltpu.SemaphoreType.DMA((XS,)),
                pltpu.SemaphoreType.DMA((4,)),
            ],
            compiler_params=pltpu.CompilerParams(
                collective_id=0, has_side_effects=True, vmem_limit_bytes=56 << 20
            ),
        )(
            prompt,
            norm_gain,
            in_weight[0].transpose(1, 0, 2),
            feat_taps[0].reshape(9, 1, local),
            fir_taps[0].T,
            residues[0],
            decay[0],
        )
        return out[None]

    return jax.shard_map(
        body,
        mesh=mesh,
        in_specs=(
            P(None, "chan"),
            P("section", "chan"),
            P("section", None, None, "chan"),
            P("section", None, None, "chan"),
            P("section", None, "chan"),
            P("section", None, "chan"),
            P("section", None, "chan"),
        ),
        out_specs=P("section", None, "chan"),
        check_vma=False,
    )
```

```python
import functools

import jax
import jax.numpy as jnp
from jax import lax
from jax.experimental import pallas as pl
from jax.experimental.pallas import tpu as pltpu
from jax.sharding import PartitionSpec as P

MESH = pl.DeviceIdType.MESH
EPSILON = 1e-06
BLOCK = 24
XS = 4
LOOK = 0
DEPTH = 2
ORDER = (0, 7, 6, 5, 4, 3, 2, 1)
UNROLL = 4
MERGE = ((0,), (1, 2), (3, 4), (5, 6), (7,))
CUTS = ((0, 3), (3, 5), (5, 7), (7, 8))


def ring_offsets(zs):
    offs = [0]
    for d in range(1, zs // 2 + 1):
        offs.append(d)
        if zs - d != d:
            offs.append(zs - d)
    return offs


def kernel(
    dims,
    prompt_ref, gain_ref, w_hbm, taps_ref, fir_ref, res_ref, decay_ref,
    o_ref,
    wbuf, xbuf, gbuf, gown, pbuf, fpad, gpad, tbuf, rhs,
    wsem, zsem, xsem, gsem, ssem,
):
    secs, zs, length = dims
    rows = BLOCK
    nblk = length // rows
    width = zs * XS * 256
    offs = ring_offsets(zs)
    sec = lax.axis_index("section")
    chan = lax.axis_index("chan")
    z = chan // XS
    x = lax.rem(chan, XS)

    def z_at(delta):
        return lax.rem(z + delta + 2 * zs, zs)

    def x_at(delta):
        return lax.rem(x + delta + 2 * XS, XS)

    def dev(s, zi, xi):
        return (s, zi * XS + xi)

    def w_copy(xr, k):
        chunk = z_at(offs[k]) * XS + x_at(xr)
        start = pl.multiple_of(chunk * 256, 256)
        return pltpu.make_async_copy(
            w_hbm.at[:, pl.ds(start, 256), :],
            wbuf.at[:, xr, pl.ds(k * 256, 256), :],
            wsem.at[xr],
        )

    gown[...] = gain_ref[...].astype(jnp.float32)

    barrier = pltpu.get_barrier_semaphore()

    def hello(s, zi, xi):
        pl.semaphore_signal(barrier, inc=1, device_id=dev(s, zi, xi), device_id_type=MESH)

    for k in range(1, zs):
        hello(sec, z_at(offs[k]), x)
    for xr in range(1, XS):
        hello(sec, z, x_at(xr))

    @pl.when(sec == 0)
    def _():
        for k in range(zs):
            hello(1, z_at(offs[k]), x)

    @pl.when(sec > 0)
    def _():
        for k in range(zs):
            hello(sec - 1, z_at(offs[k]), x)

    for xr in range(XS):
        for k in range(zs):
            w_copy(xr, k).start()

    greetings = zs - 1 + XS - 1
    greetings = greetings + jnp.where(sec < secs - 1, zs, 0)
    greetings = greetings + jnp.where(sec == 1, zs, 0)
    pl.semaphore_wait(barrier, greetings)

    column = [z_at(-offs[k]) * XS + x for k in range(zs)]
    across = [z * XS + x_at(-xr) for xr in range(XS)]

    def send_block(src, target, b, own):
        for k in ORDER:
            dst, sem = xbuf.at[b, 0, k], zsem.at[b, k]
            if own and k == 0:
                pltpu.make_async_copy(src, dst, sem).start()
            else:
                pltpu.make_async_remote_copy(
                    src_ref=src, dst_ref=dst, send_sem=ssem.at[0], recv_sem=sem,
                    device_id=(target, column[k]), device_id_type=MESH,
                ).start()

    pltpu.make_async_copy(gown, gbuf.at[0, 0], gsem.at[0]).start()
    for k in range(1, zs):
        pltpu.make_async_remote_copy(
            src_ref=gown, dst_ref=gbuf.at[0, k], send_sem=ssem.at[2], recv_sem=gsem.at[0],
            device_id=dev(sec, z_at(-offs[k]), x), device_id_type=MESH,
        ).start()

    @pl.when(sec == 0)
    def _():
        send_block(prompt_ref.at[0], 0, 0, True)

    @pl.when(sec == 1)
    def _():
        @pl.loop(1, nblk)
        def _(b):
            send_block(prompt_ref.at[b], 0, b, False)

    pad = rows
    fpad[...] = jnp.zeros_like(fpad)
    medium = lax.rem(sec, 2) == 0

    @pl.when(medium)
    def _():
        spread = (
            lax.broadcasted_iota(jnp.int32, (16, 128), 0)
            == lax.rem(lax.broadcasted_iota(jnp.int32, (16, 128), 1), 16)
        ).astype(jnp.float32)
        taps = lax.dot_general(
            fir_ref[...], spread, (((0,), (0,)), ((), ())),
            precision=lax.Precision.HIGHEST, preferred_element_type=jnp.float32,
        )
        count = min(fir_ref.shape[1], length)
        fpad[pl.ds(pad, count), :] = taps[:count]

    @pl.when(jnp.logical_not(medium))
    def _():
        lags = lax.broadcasted_iota(jnp.int32, (length, 128), 0).astype(jnp.float32)
        res = jnp.concatenate([res_ref[...]] * 8, axis=1)
        rate = jnp.concatenate([decay_ref[...]] * 8, axis=1)
        total = jnp.zeros((length, 128), jnp.float32)
        for n in range(res.shape[0]):
            total = total + res[n : n + 1] * jnp.exp(-rate[n : n + 1] * lags)
        fpad[pl.ds(pad, length), :] = total

    span = length + rows - 8
    lane_row = lax.broadcasted_iota(jnp.int32, (1, 128), 1) // 16
    shifted = jnp.zeros((span, 128), jnp.float32)
    for i in range(8):
        shifted = jnp.where(lane_row == i, fpad[pl.ds(8 - i, span), :], shifted)
    gpad[...] = shifted
    for d in range(nblk):
        for q in range(rows // 8):
            lo = d * rows - 8 * q + rows - 8
            tbuf[d, :, pl.ds(q * 128, 128)] = gpad[pl.ds(lo, rows), :].astype(jnp.bfloat16)

    for d in range(UNROLL - 1):
        tbuf[nblk + d] = jnp.zeros(tbuf.shape[1:], jnp.bfloat16)
        rhs[d] = jnp.zeros(rhs.shape[1:], jnp.bfloat16)
    pbuf[...] = jnp.zeros_like(pbuf)

    def forward(b):
        for group in MERGE:
            for k in group:
                pltpu.make_async_copy(xbuf.at[b, 0, k], xbuf.at[b, 0, k], zsem.at[b, k]).wait()
            cut = [lo <= group[0] < hi for lo, hi in CUTS].index(True)
            part = pl.ds(group[0], len(group))
            for xr in (2, 1, 3):
                pltpu.make_async_remote_copy(
                    src_ref=xbuf.at[b, 0, part], dst_ref=xbuf.at[b, xr, part],
                    send_sem=ssem.at[1], recv_sem=xsem.at[b, xr - 1, cut],
                    device_id=(sec, across[xr]), device_id_type=MESH,
                ).start()

    def forward_next(b, place):
        if place == LOOK:
            then = b + jnp.where(sec == 0, DEPTH, 1)

            @pl.when(then < nblk)
            def _():
                forward(then)

    def product(b, xr, lo, hi, acc, squares):
        pieces = []
        for k in range(lo, hi):
            piece = xbuf[b, xr, k].astype(jnp.float32)
            square = piece * piece
            squares = squares + (square[:, :128] + square[:, 128:])
            pieces.append((piece * gbuf[xr, k]).astype(jnp.bfloat16))
        left = jnp.concatenate(pieces, axis=1)
        return (
            tuple(
                acc[i] + jnp.dot(
                    left, wbuf[i, xr, pl.ds(lo * 256, (hi - lo) * 256), :],
                    preferred_element_type=jnp.float32,
                )
                for i in range(3)
            ),
            squares,
        )

    lane_group = lax.broadcasted_iota(jnp.int32, (16, 256), 1) // 16
    own_group = lane_group == lax.broadcasted_iota(jnp.int32, (16, 256), 0)

    pltpu.make_async_copy(gbuf.at[0], gbuf.at[0], gsem.at[0]).wait()
    for xr in range(1, XS):
        pltpu.make_async_remote_copy(
            src_ref=gbuf.at[0], dst_ref=gbuf.at[xr], send_sem=ssem.at[3], recv_sem=gsem.at[xr],
            device_id=dev(sec, z, x_at(-xr)), device_id_type=MESH,
        ).start()

    forward(0)

    @pl.when(sec == 0)
    def _():
        for b in range(1, min(DEPTH, nblk)):
            forward(b)

    for xr in range(XS):
        pltpu.make_async_copy(wbuf.at[:, xr], wbuf.at[:, xr], wsem.at[xr]).wait()
    for xr in range(1, XS):
        pltpu.make_async_copy(gbuf.at[xr], gbuf.at[xr], gsem.at[xr]).wait()

    def block(b, carry):
        def earlier(step, total):
            for i in range(UNROLL):
                d = 1 + step * UNROLL + i
                total = total + jnp.dot(
                    tbuf[d], rhs[b - d + UNROLL - 1], preferred_element_type=jnp.float32
                )
            return total

        conv = lax.fori_loop(
            0, (b + UNROLL - 1) // UNROLL, earlier, jnp.zeros((rows, 256), jnp.float32)
        )
        acc = tuple(jnp.zeros((rows, 256), jnp.float32) for i in range(3))
        state = product(b, 0, 0, zs, acc, jnp.zeros((rows, 128), jnp.float32))
        forward_next(b, 0)
        for cut, (lo, hi) in enumerate(CUTS):
            for xr in (1, 3, 2):
                part = xbuf.at[b, xr, pl.ds(lo, hi - lo)]
                pltpu.make_async_copy(part, part, xsem.at[b, xr - 1, cut]).wait()
                state = product(b, xr, lo, hi, *state)
        acc, squares = state
        scale = lax.rsqrt(jnp.sum(squares, axis=1, keepdims=True) / width + EPSILON)
        feats = []
        for i in range(3):
            pbuf[i, pl.ds(8, rows), :] = acc[i] * scale
            feats.append(
                taps_ref[i] * pbuf[i, pl.ds(8, rows), :]
                + taps_ref[3 + i] * pbuf[i, pl.ds(7, rows), :]
                + taps_ref[6 + i] * pbuf[i, pl.ds(6, rows), :]
            )
        kv = feats[1] * feats[2]
        for p in range(rows):
            rhs[b + UNROLL - 1, pl.ds(p * 16, 16), :] = jnp.where(
                own_group, jnp.broadcast_to(kv[p : p + 1], (16, 256)), 0.0
            ).astype(jnp.bfloat16)
        conv = conv + jnp.dot(tbuf[0], rhs[b + UNROLL - 1], preferred_element_type=jnp.float32)
        result = xbuf[b, 0, 0].astype(jnp.float32) + feats[0] * conv
        o_ref[b] = result.astype(jnp.bfloat16)

        @pl.when(sec < secs - 1)
        def _():
            send_block(o_ref.at[b], sec + 1, b, False)

        for i in range(3):
            pbuf[i, pl.ds(0, 8), :] = pbuf[i, pl.ds(rows, 8), :]

        forward_next(b, 4)
        return carry

    lax.fori_loop(0, nblk, block, 0)

    def sent(view, which):
        pltpu.make_async_copy(view, view, ssem.at[which]).wait()

    @pl.when(sec == 0)
    def _():
        sent(xbuf.at[0, 0, pl.ds(1, zs - 1)], 0)

    @pl.when(sec == 1)
    def _():
        sent(xbuf.at[pl.ds(1, nblk - 1), 0], 0)

    @pl.when(sec < secs - 1)
    def _():
        sent(xbuf.at[:, 0], 0)

    sent(xbuf.at[:, pl.ds(1, XS - 1)], 1)
    sent(gbuf.at[0, pl.ds(1, zs - 1)], 2)
    sent(gbuf.at[pl.ds(1, XS - 1)], 3)


def solution(mesh):
    secs = mesh.shape["section"]
    zs = mesh.shape["chan"] // XS

    def body(prompt, norm_gain, in_weight, feat_taps, fir_taps, residues, decay):
        length, local = prompt.shape
        rows = BLOCK
        nblk = length // rows
        vmem = pl.BlockSpec(memory_space=pltpu.VMEM)
        out = pl.pallas_call(
            functools.partial(kernel, (secs, zs, length)),
            name="relay",
            out_shape=jax.ShapeDtypeStruct((nblk, rows, local), jnp.bfloat16),
            in_specs=[vmem, vmem, pl.BlockSpec(memory_space=pl.ANY), vmem, vmem, vmem, vmem],
            out_specs=vmem,
            scratch_shapes=[
                pltpu.VMEM((3, XS, zs * 256, 256), jnp.bfloat16),
                pltpu.VMEM((nblk, XS, zs, rows, 256), jnp.bfloat16),
                pltpu.VMEM((XS, zs, 1, 256), jnp.float32),
                pltpu.VMEM((1, 256), jnp.float32),
                pltpu.VMEM((3, 8 + rows, 256), jnp.float32),
                pltpu.VMEM((rows + length, 128), jnp.float32),
                pltpu.VMEM((rows + length - 8, 128), jnp.float32),
                pltpu.VMEM((nblk + UNROLL - 1, rows, rows * 16), jnp.bfloat16),
                pltpu.VMEM((nblk + UNROLL - 1, rows * 16, 256), jnp.bfloat16),
                pltpu.SemaphoreType.DMA((XS,)),
                pltpu.SemaphoreType.DMA((nblk, zs)),
                pltpu.SemaphoreType.DMA((nblk, XS - 1, len(CUTS))),
                pltpu.SemaphoreType.DMA((XS,)),
                pltpu.SemaphoreType.DMA((4,)),
            ],
            compiler_params=pltpu.CompilerParams(
                collective_id=0, has_side_effects=True, vmem_limit_bytes=56 << 20
            ),
        )(
            prompt.reshape(nblk, rows, local),
            norm_gain,
            in_weight[0].transpose(1, 0, 2),
            feat_taps[0].reshape(9, 1, local),
            fir_taps[0].T,
            residues[0],
            decay[0],
        )
        return out.reshape(1, length, local)

    return jax.shard_map(
        body,
        mesh=mesh,
        in_specs=(
            P(None, "chan"),
            P("section", "chan"),
            P("section", None, None, "chan"),
            P("section", None, None, "chan"),
            P("section", None, "chan"),
            P("section", None, "chan"),
            P("section", None, "chan"),
        ),
        out_specs=P("section", None, "chan"),
        check_vma=False,
    )
```

```python
import functools

import jax
import jax.numpy as jnp
from jax import lax
from jax.experimental import pallas as pl
from jax.experimental.pallas import tpu as pltpu
from jax.sharding import PartitionSpec as P

MESH = pl.DeviceIdType.MESH
EPSILON = 1e-06
BLOCK = 24
XS = 4
LOOK = 0
DEPTH = 3
ORDER = (0, 7, 6, 5, 4, 3, 2, 1)
UNROLL = 4
MERGE = ((0,), (1, 2), (3, 4), (5, 6), (7,))
CUTS = ((0, 3), (3, 5), (5, 7), (7, 8))


def ring_offsets(zs):
    offs = [0]
    for d in range(1, zs // 2 + 1):
        offs.append(d)
        if zs - d != d:
            offs.append(zs - d)
    return offs


def kernel(
    dims,
    prompt_ref, gain_ref, w_hbm, taps_ref, fir_ref, res_ref, decay_ref,
    o_ref,
    wbuf, xbuf, gbuf, gown, pbuf, fpad, gpad, tbuf, rhs,
    wsem, zsem, xsem, gsem, ssem,
):
    secs, zs, length = dims
    rows = BLOCK
    nblk = length // rows
    width = zs * XS * 256
    offs = ring_offsets(zs)
    sec = lax.axis_index("section")
    chan = lax.axis_index("chan")
    z = chan // XS
    x = lax.rem(chan, XS)

    def z_at(delta):
        return lax.rem(z + delta + 2 * zs, zs)

    def x_at(delta):
        return lax.rem(x + delta + 2 * XS, XS)

    def dev(s, zi, xi):
        return (s, zi * XS + xi)

    def w_copy(xr, k):
        chunk = z_at(offs[k]) * XS + x_at(xr)
        start = pl.multiple_of(chunk * 256, 256)
        return pltpu.make_async_copy(
            w_hbm.at[:, pl.ds(start, 256), :],
            wbuf.at[:, xr, pl.ds(k * 256, 256), :],
            wsem.at[xr],
        )

    gown[...] = gain_ref[...].astype(jnp.float32)

    barrier = pltpu.get_barrier_semaphore()

    def hello(s, zi, xi):
        pl.semaphore_signal(barrier, inc=1, device_id=dev(s, zi, xi), device_id_type=MESH)

    for k in range(1, zs):
        hello(sec, z_at(offs[k]), x)
    for xr in range(1, XS):
        hello(sec, z, x_at(xr))

    @pl.when(sec == 0)
    def _():
        for k in range(zs):
            hello(1, z_at(offs[k]), x)

    @pl.when(sec > 0)
    def _():
        for k in range(zs):
            hello(sec - 1, z_at(offs[k]), x)

    for xr in range(XS):
        for k in range(zs):
            w_copy(xr, k).start()

    greetings = zs - 1 + XS - 1
    greetings = greetings + jnp.where(sec < secs - 1, zs, 0)
    greetings = greetings + jnp.where(sec == 1, zs, 0)
    pl.semaphore_wait(barrier, greetings)

    column = [z_at(-offs[k]) * XS + x for k in range(zs)]
    across = [z * XS + x_at(-xr) for xr in range(XS)]

    def send_block(src, target, b, own):
        for k in ORDER:
            dst, sem = xbuf.at[b, 0, k], zsem.at[b, k]
            if own and k == 0:
                pltpu.make_async_copy(src, dst, sem).start()
            else:
                pltpu.make_async_remote_copy(
                    src_ref=src, dst_ref=dst, send_sem=ssem.at[0], recv_sem=sem,
                    device_id=(target, column[k]), device_id_type=MESH,
                ).start()

    pltpu.make_async_copy(gown, gbuf.at[0, 0], gsem.at[0]).start()
    for k in range(1, zs):
        pltpu.make_async_remote_copy(
            src_ref=gown, dst_ref=gbuf.at[0, k], send_sem=ssem.at[2], recv_sem=gsem.at[0],
            device_id=dev(sec, z_at(-offs[k]), x), device_id_type=MESH,
        ).start()

    @pl.when(sec == 0)
    def _():
        send_block(prompt_ref.at[0], 0, 0, True)

    @pl.when(sec == 1)
    def _():
        @pl.loop(1, nblk)
        def _(b):
            send_block(prompt_ref.at[b], 0, b, False)

    pad = rows
    fpad[...] = jnp.zeros_like(fpad)
    medium = lax.rem(sec, 2) == 0

    @pl.when(medium)
    def _():
        spread = (
            lax.broadcasted_iota(jnp.int32, (16, 128), 0)
            == lax.rem(lax.broadcasted_iota(jnp.int32, (16, 128), 1), 16)
        ).astype(jnp.float32)
        taps = lax.dot_general(
            fir_ref[...], spread, (((0,), (0,)), ((), ())),
            precision=lax.Precision.HIGHEST, preferred_element_type=jnp.float32,
        )
        count = min(fir_ref.shape[1], length)
        fpad[pl.ds(pad, count), :] = taps[:count]

    @pl.when(jnp.logical_not(medium))
    def _():
        lags = lax.broadcasted_iota(jnp.int32, (length, 128), 0).astype(jnp.float32)
        res = jnp.concatenate([res_ref[...]] * 8, axis=1)
        rate = jnp.concatenate([decay_ref[...]] * 8, axis=1)
        total = jnp.zeros((length, 128), jnp.float32)
        for n in range(res.shape[0]):
            total = total + res[n : n + 1] * jnp.exp(-rate[n : n + 1] * lags)
        fpad[pl.ds(pad, length), :] = total

    span = length + rows - 8
    lane_row = lax.broadcasted_iota(jnp.int32, (1, 128), 1) // 16
    shifted = jnp.zeros((span, 128), jnp.float32)
    for i in range(8):
        shifted = jnp.where(lane_row == i, fpad[pl.ds(8 - i, span), :], shifted)
    gpad[...] = shifted
    for d in range(nblk):
        for q in range(rows // 8):
            lo = d * rows - 8 * q + rows - 8
            tbuf[d, :, pl.ds(q * 128, 128)] = gpad[pl.ds(lo, rows), :].astype(jnp.bfloat16)

    for d in range(UNROLL - 1):
        tbuf[nblk + d] = jnp.zeros(tbuf.shape[1:], jnp.bfloat16)
        rhs[d] = jnp.zeros(rhs.shape[1:], jnp.bfloat16)
    pbuf[...] = jnp.zeros_like(pbuf)

    def forward(b):
        for group in MERGE:
            for k in group:
                pltpu.make_async_copy(xbuf.at[b, 0, k], xbuf.at[b, 0, k], zsem.at[b, k]).wait()
            cut = [lo <= group[0] < hi for lo, hi in CUTS].index(True)
            part = pl.ds(group[0], len(group))
            for xr in (1, 3, 2):
                pltpu.make_async_remote_copy(
                    src_ref=xbuf.at[b, 0, part], dst_ref=xbuf.at[b, xr, part],
                    send_sem=ssem.at[1], recv_sem=xsem.at[b, xr - 1, cut],
                    device_id=(sec, across[xr]), device_id_type=MESH,
                ).start()

    def forward_next(b, place):
        if place == LOOK:
            then = b + jnp.where(sec == 0, DEPTH, 1)

            @pl.when(then < nblk)
            def _():
                forward(then)

    def product(b, xr, lo, hi, acc, squares):
        pieces = []
        for k in range(lo, hi):
            piece = xbuf[b, xr, k].astype(jnp.float32)
            square = piece * piece
            squares = squares + (square[:, :128] + square[:, 128:])
            pieces.append((piece * gbuf[xr, k]).astype(jnp.bfloat16))
        left = jnp.concatenate(pieces, axis=1)
        return (
            tuple(
                acc[i] + jnp.dot(
                    left, wbuf[i, xr, pl.ds(lo * 256, (hi - lo) * 256), :],
                    preferred_element_type=jnp.float32,
                )
                for i in range(3)
            ),
            squares,
        )

    lane_group = lax.broadcasted_iota(jnp.int32, (16, 256), 1) // 16
    own_group = lane_group == lax.broadcasted_iota(jnp.int32, (16, 256), 0)

    pltpu.make_async_copy(gbuf.at[0], gbuf.at[0], gsem.at[0]).wait()
    for xr in range(1, XS):
        pltpu.make_async_remote_copy(
            src_ref=gbuf.at[0], dst_ref=gbuf.at[xr], send_sem=ssem.at[3], recv_sem=gsem.at[xr],
            device_id=dev(sec, z, x_at(-xr)), device_id_type=MESH,
        ).start()

    forward(0)

    @pl.when(sec == 0)
    def _():
        for b in range(1, min(DEPTH, nblk)):
            forward(b)

    for xr in range(XS):
        pltpu.make_async_copy(wbuf.at[:, xr], wbuf.at[:, xr], wsem.at[xr]).wait()
    for xr in range(1, XS):
        pltpu.make_async_copy(gbuf.at[xr], gbuf.at[xr], gsem.at[xr]).wait()

    def block(b, carry):
        def earlier(step, total):
            for i in range(UNROLL):
                d = 1 + step * UNROLL + i
                total = total + jnp.dot(
                    tbuf[d], rhs[b - d + UNROLL - 1], preferred_element_type=jnp.float32
                )
            return total

        conv = lax.fori_loop(
            0, (b + UNROLL - 1) // UNROLL, earlier, jnp.zeros((rows, 256), jnp.float32)
        )
        acc = tuple(jnp.zeros((rows, 256), jnp.float32) for i in range(3))
        state = product(b, 0, 0, zs, acc, jnp.zeros((rows, 128), jnp.float32))
        forward_next(b, 0)
        for cut, (lo, hi) in enumerate(CUTS):
            for xr in (1, 3, 2):
                part = xbuf.at[b, xr, pl.ds(lo, hi - lo)]
                pltpu.make_async_copy(part, part, xsem.at[b, xr - 1, cut]).wait()
                state = product(b, xr, lo, hi, *state)
        acc, squares = state
        scale = lax.rsqrt(jnp.sum(squares, axis=1, keepdims=True) / width + EPSILON)
        feats = []
        for i in range(3):
            pbuf[i, pl.ds(8, rows), :] = acc[i] * scale
            feats.append(
                taps_ref[i] * pbuf[i, pl.ds(8, rows), :]
                + taps_ref[3 + i] * pbuf[i, pl.ds(7, rows), :]
                + taps_ref[6 + i] * pbuf[i, pl.ds(6, rows), :]
            )
        kv = feats[1] * feats[2]
        for p in range(rows):
            rhs[b + UNROLL - 1, pl.ds(p * 16, 16), :] = jnp.where(
                own_group, jnp.broadcast_to(kv[p : p + 1], (16, 256)), 0.0
            ).astype(jnp.bfloat16)
        conv = conv + jnp.dot(tbuf[0], rhs[b + UNROLL - 1], preferred_element_type=jnp.float32)
        result = xbuf[b, 0, 0].astype(jnp.float32) + feats[0] * conv
        o_ref[b] = result.astype(jnp.bfloat16)

        @pl.when(sec < secs - 1)
        def _():
            send_block(o_ref.at[b], sec + 1, b, False)

        for i in range(3):
            pbuf[i, pl.ds(0, 8), :] = pbuf[i, pl.ds(rows, 8), :]

        forward_next(b, 4)
        return carry

    lax.fori_loop(0, nblk, block, 0)

    def sent(view, which):
        pltpu.make_async_copy(view, view, ssem.at[which]).wait()

    @pl.when(sec == 0)
    def _():
        sent(xbuf.at[0, 0, pl.ds(1, zs - 1)], 0)

    @pl.when(sec == 1)
    def _():
        sent(xbuf.at[pl.ds(1, nblk - 1), 0], 0)

    @pl.when(sec < secs - 1)
    def _():
        sent(xbuf.at[:, 0], 0)

    sent(xbuf.at[:, pl.ds(1, XS - 1)], 1)
    sent(gbuf.at[0, pl.ds(1, zs - 1)], 2)
    sent(gbuf.at[pl.ds(1, XS - 1)], 3)


def solution(mesh):
    secs = mesh.shape["section"]
    zs = mesh.shape["chan"] // XS

    def body(prompt, norm_gain, in_weight, feat_taps, fir_taps, residues, decay):
        length, local = prompt.shape
        rows = BLOCK
        nblk = length // rows
        vmem = pl.BlockSpec(memory_space=pltpu.VMEM)
        out = pl.pallas_call(
            functools.partial(kernel, (secs, zs, length)),
            name="relay",
            out_shape=jax.ShapeDtypeStruct((nblk, rows, local), jnp.bfloat16),
            in_specs=[vmem, vmem, pl.BlockSpec(memory_space=pl.ANY), vmem, vmem, vmem, vmem],
            out_specs=vmem,
            scratch_shapes=[
                pltpu.VMEM((3, XS, zs * 256, 256), jnp.bfloat16),
                pltpu.VMEM((nblk, XS, zs, rows, 256), jnp.bfloat16),
                pltpu.VMEM((XS, zs, 1, 256), jnp.float32),
                pltpu.VMEM((1, 256), jnp.float32),
                pltpu.VMEM((3, 8 + rows, 256), jnp.float32),
                pltpu.VMEM((rows + length, 128), jnp.float32),
                pltpu.VMEM((rows + length - 8, 128), jnp.float32),
                pltpu.VMEM((nblk + UNROLL - 1, rows, rows * 16), jnp.bfloat16),
                pltpu.VMEM((nblk + UNROLL - 1, rows * 16, 256), jnp.bfloat16),
                pltpu.SemaphoreType.DMA((XS,)),
                pltpu.SemaphoreType.DMA((nblk, zs)),
                pltpu.SemaphoreType.DMA((nblk, XS - 1, len(CUTS))),
                pltpu.SemaphoreType.DMA((XS,)),
                pltpu.SemaphoreType.DMA((4,)),
            ],
            compiler_params=pltpu.CompilerParams(
                collective_id=0, has_side_effects=True, vmem_limit_bytes=56 << 20
            ),
        )(
            prompt.reshape(nblk, rows, local),
            norm_gain,
            in_weight[0].transpose(1, 0, 2),
            feat_taps[0].reshape(9, 1, local),
            fir_taps[0].T,
            residues[0],
            decay[0],
        )
        return out.reshape(1, length, local)

    return jax.shard_map(
        body,
        mesh=mesh,
        in_specs=(
            P(None, "chan"),
            P("section", "chan"),
            P("section", None, None, "chan"),
            P("section", None, None, "chan"),
            P("section", None, "chan"),
            P("section", None, "chan"),
            P("section", None, "chan"),
        ),
        out_specs=P("section", None, "chan"),
        check_vma=False,
    )
```
